32 devices in a mesh: seq: 8 (over z, y), head: 4 (over x, core).
Axes of the slice: x: 2, y: 2, z: 4, core: 2. Of those that a mesh axis runs over, the one named last changes fastest.
Arguments:
- tokens: bfloat16 [4096, 4096], P('seq', 'head'), may hold values from -54 to 54
- w_query: bfloat16 [4096, 4096], P('seq', 'head'), may hold values from -0.09375 to 0.09375
- w_key: bfloat16 [4096, 1024], P('seq', 'head'), may hold values from -0.09375 to 0.09375
- w_value: bfloat16 [4096, 1024], P('seq', 'head'), may hold values from -0.09375 to 0.09375
Outputs:
- attended: bfloat16 [4096, 4096], P('seq', 'head')
The draws below stay inside these ranges and needn't reach their ends.
All inputs are finite; a program needn't handle non-finite values.
Results may differ from the reference program's by a relative error of at most 0.0055.
The reference program's roundings to bfloat16 on the way (of `query` and `weight`) count: a program that leaves them out, or rounds other values in their place, can miss the bound.
Values may be sent and summed in bfloat16 or wider, within the bound.
No kernel may reach another device: no remote copies, remote signals or barrier semaphores. Data moves between devices by JAX's collectives and lax.ppermute only.
A program may use at most 64 MiB of HBM per device.

```python
import jax
import jax.numpy as jnp
from jax import lax

D = 4096
HEADS = 32
KV_HEADS = 8
HEAD_DIM = 128
BLOCK = 512
TOKENS = 4096


def draw_tokens(key, part):
    base = jax.random.normal(jax.random.fold_in(key, 11), (TOKENS, D), jnp.float32)
    values = jnp.clip(base, -6.0, 6.0)
    return values.astype(jnp.bfloat16)


def block_levels(rng, dims, shards, smallest, largest):
    def one(dim, shards_of):
        heights = jax.random.uniform(jax.random.fold_in(jax.random.fold_in(rng, 6), dim), (shards_of,), jnp.float32, smallest / len(shards), largest / len(shards))
        return jnp.repeat(jnp.exp(heights), dims[dim] // shards_of).reshape((-1,) + (1,) * (len(dims) - dim - 1))

    level = one(*shards[0])
    for cut in shards[1:]:
        level = level * one(*cut)
    return level


def normal_values(rng, shape, width, reach, split=(), kind=jnp.bfloat16):
    gain = block_levels(rng, shape, split, -0.22, 0.18) if split else 1.0
    values = jax.random.normal(rng, shape, jnp.float32) * width * gain
    return jnp.minimum(jnp.maximum(values, -reach), reach).astype(kind)


def setup_inputs(seed: int = 0) -> dict:
    streams_of = jax.random.split(jax.random.key(seed), 5)
    return {
        "tokens": draw_tokens(jax.random.fold_in(streams_of[4], 71), 0),
        "w_query": normal_values(streams_of[1], (D, HEADS * HEAD_DIM), D ** -0.5, 0.09375, ((0, 8), (1, 4))),
        "w_key": normal_values(streams_of[2], (D, KV_HEADS * HEAD_DIM), D ** -0.5, 0.09375, ((0, 8), (1, 4))),
        "w_value": normal_values(streams_of[3], (D, KV_HEADS * HEAD_DIM), D ** -0.5, 0.09375, ((0, 8), (1, 4))),
    }


def reference(tokens, w_query, w_key, w_value):
    query = jnp.dot(tokens, w_query, preferred_element_type=jnp.float32).astype(jnp.bfloat16)
    key = jnp.dot(tokens, w_key, preferred_element_type=jnp.float32).astype(jnp.bfloat16)
    value = jnp.dot(tokens, w_value, preferred_element_type=jnp.float32).astype(jnp.bfloat16)
    blocks = TOKENS // BLOCK
    group = HEADS // KV_HEADS
    gaps = []
    step = 1
    while step < blocks:
        gaps.append(step)
        step = step * 2
    query_all = query.reshape(blocks, BLOCK, KV_HEADS, group, HEAD_DIM)
    key_all = key.reshape(blocks, BLOCK, KV_HEADS, HEAD_DIM)
    value_all = value.reshape(blocks, BLOCK, KV_HEADS, HEAD_DIM)
    rows = lax.broadcasted_iota(jnp.int32, (BLOCK, BLOCK), 0)
    cols = lax.broadcasted_iota(jnp.int32, (BLOCK, BLOCK), 1)
    causal = rows >= cols
    scale = HEAD_DIM ** -0.5

    def one_block(index):
        local_q = lax.dynamic_index_in_dim(query_all, index, 0, keepdims=False).astype(jnp.float32)
        key_list = [lax.dynamic_index_in_dim(key_all, index, 0, keepdims=False)]
        value_list = [lax.dynamic_index_in_dim(value_all, index, 0, keepdims=False)]
        masks = [causal]
        for gap in gaps:
            source = jnp.maximum(index - gap, 0).astype(jnp.int32)
            key_list.append(lax.dynamic_index_in_dim(key_all, source, 0, keepdims=False))
            value_list.append(lax.dynamic_index_in_dim(value_all, source, 0, keepdims=False))
            masks.append(jnp.broadcast_to(index >= gap, (BLOCK, BLOCK)))
        keys = jnp.concatenate(key_list, axis=0).astype(jnp.float32)
        values = jnp.concatenate(value_list, axis=0).astype(jnp.float32)
        visible = jnp.concatenate(masks, axis=1)
        score = jnp.einsum('qkgd,skd->kgqs', local_q, keys) * scale
        score = jnp.where(visible[None, None], score, -jnp.inf)
        peak = jnp.max(score, axis=-1, keepdims=True)
        raw = jnp.exp(score - peak)
        total = jnp.sum(raw, axis=-1)
        weight = raw.astype(jnp.bfloat16).astype(jnp.float32)
        summed = jnp.einsum('kgqs,skd->qkgd', weight, values)
        normed = summed / jnp.transpose(total, (2, 0, 1))[..., None]
        return normed.reshape(BLOCK, HEADS * HEAD_DIM).astype(jnp.bfloat16)

    result = lax.map(one_block, jnp.arange(blocks, dtype=jnp.int32))
    return result.reshape(TOKENS, HEADS * HEAD_DIM)
```

```python
import functools
import math

import jax
import jax.numpy as jnp
from jax import lax
from jax.experimental import pallas as pl
from jax.experimental.pallas import tpu as pltpu
from jax.sharding import PartitionSpec as P

HEAD_DIM = 128


def from_behind(value, axis, by):
    count = lax.axis_size(axis)
    pairs = [(i, i + by) for i in range(count) if 0 <= i + by < count]
    return lax.ppermute(value, axis, pairs)


def plain_body(tokens, w_query, w_key, w_value):
    whole = lax.all_gather(tokens, "head", axis=1, tiled=True)
    rows = whole.shape[0]
    pieces = (
        lax.all_gather(w_query, "seq", axis=0, tiled=True),
        lax.all_gather(w_key, "seq", axis=0, tiled=True),
        lax.all_gather(w_value, "seq", axis=0, tiled=True),
    )
    query, key, value = tuple(
        jnp.dot(whole, piece, preferred_element_type=jnp.float32).astype(jnp.bfloat16) for piece in pieces
    )
    local_kv = key.shape[1] // HEAD_DIM
    local_heads = query.shape[1] // HEAD_DIM
    group = local_heads // local_kv
    query_four = query.reshape(rows, local_kv, group, HEAD_DIM)
    levels = (lax.axis_size("seq") - 1).bit_length()
    myself = lax.axis_index("seq")
    row_ids = lax.broadcasted_iota(jnp.int32, (rows, rows), 0)
    col_ids = lax.broadcasted_iota(jnp.int32, (rows, rows), 1)
    entries = [(key, value, row_ids >= col_ids)]
    for level in range(levels):
        far_key, far_value = from_behind((key, value), "seq", 2**level)
        entries.append((far_key, far_value, jnp.broadcast_to(myself >= 2**level, (rows, rows))))
    scale = HEAD_DIM ** (-0.5)

    def scores(key_piece, visible):
        key_three = key_piece.reshape(rows, local_kv, HEAD_DIM)
        raw = jnp.einsum("qkgd,skd->kgqs", query_four, key_three, preferred_element_type=jnp.float32) * scale
        return jnp.where(visible[None, None], raw, -jnp.inf)

    score_list = [scores(key_piece, visible) for key_piece, value_piece, visible in entries]
    peak = jnp.full((local_kv, group, rows), -jnp.inf, jnp.float32)
    for score in score_list:
        peak = jnp.maximum(peak, jnp.max(score, axis=-1))
    total = jnp.zeros((local_kv, group, rows), jnp.float32)
    summed = jnp.zeros((rows, local_kv, group, HEAD_DIM), jnp.float32)
    for score, entry in zip(score_list, entries):
        expo = jnp.exp(score - peak[..., None])
        total = total + jnp.sum(expo, axis=-1)
        weight = expo.astype(jnp.bfloat16)
        value_three = entry[1].reshape(rows, local_kv, HEAD_DIM)
        summed = summed + jnp.einsum("kgqs,skd->qkgd", weight, value_three, preferred_element_type=jnp.float32)
    normed = summed / jnp.transpose(total, (2, 0, 1))[..., None]
    return normed.reshape(rows, local_heads * HEAD_DIM).astype(jnp.bfloat16)


def flip(value, axis, mask):
    return lax.ppermute(value, axis, [(i, i ^ mask) for i in range(lax.axis_size(axis))])


def shift(value, axis, by, keep):
    count = lax.axis_size(axis)
    return lax.ppermute(value, axis, [(i, i + by) for i in range(count) if i + by < count and keep(i)])


def project_kernel(pieces, idx, *refs):
    xs = refs[: 2 * pieces]
    ws = refs[2 * pieces : -4]
    out, x_all, w_all, sems = refs[-4:]
    s, h = idx[0], idx[1]
    rows, width = xs[0].shape
    depth = ws[0].shape[0]
    bit = lax.rem(s // 2, 2)
    w_copies, x_copies = [], []
    for m, ref in enumerate(ws):
        dst = w_all.at[pl.ds(pl.multiple_of((s ^ m) * depth, depth), depth), :]
        w_copies.append(pltpu.make_async_copy(ref, dst, sems.at[m]))
    for k, ref in enumerate(xs):
        block, j = divmod(k, pieces)
        row = pl.multiple_of((bit ^ block) * rows, rows)
        col = pl.multiple_of((h ^ j) * width, width)
        dst = x_all.at[pl.ds(row, rows), pl.ds(col, width)]
        x_copies.append(pltpu.make_async_copy(ref, dst, sems.at[len(ws) + k]))
    for copy in w_copies + x_copies:
        copy.start()
    for copy in w_copies:
        copy.wait()
    tile = min(256, rows)
    for block in range(2):
        for copy in x_copies[block * pieces : (block + 1) * pieces]:
            copy.wait()
        first = pl.multiple_of((bit ^ block) * rows, rows)

        def step(i, carry):
            at = pl.ds(pl.multiple_of(first + i * tile, tile), tile)
            out[at, :] = jnp.dot(x_all[at, :], w_all[...], preferred_element_type=jnp.float32).astype(out.dtype)
            return carry

        lax.fori_loop(0, rows // tile, step, 0)


def project(idx, xs, ws):
    pieces = len(xs) // 2
    rows, width = xs[0].shape
    depth, cols = ws[0].shape
    total = depth * len(ws)
    spec = pl.BlockSpec(memory_space=pl.ANY)
    return pl.pallas_call(
        functools.partial(project_kernel, pieces),
        out_shape=jax.ShapeDtypeStruct((2 * rows, cols), jnp.bfloat16),
        grid_spec=pltpu.PrefetchScalarGridSpec(
            num_scalar_prefetch=1,
            grid=(1,),
            in_specs=[spec] * (len(xs) + len(ws)),
            out_specs=pl.BlockSpec((2 * rows, cols), lambda i, idx: (0, 0)),
            scratch_shapes=[
                pltpu.VMEM((2 * rows, total), jnp.bfloat16),
                pltpu.VMEM((total, cols), jnp.bfloat16),
                pltpu.SemaphoreType.DMA((len(xs) + len(ws),)),
            ],
        ),
        compiler_params=pltpu.CompilerParams(vmem_limit_bytes=32 << 20),
        cost_estimate=pl.CostEstimate(
            flops=4 * rows * total * cols,
            bytes_accessed=2 * (2 * rows * total + total * cols + 2 * rows * cols),
            transcendentals=0,
        ),
    )(idx, *xs, *ws)


def attend_kernel(heads, per_kv, levels, idx, q, own, side, diag, *refs):
    out = refs[-1]
    far = refs[:-1]
    s, zb = idx[0], idx[1]
    rows = out.shape[0]
    y = lax.rem(s, 2)
    b = (s // 4) * 4 + 2 * zb + y
    kv_cols = own.shape[1] // 2

    def rows_of(ref, which, col):
        return ref[pl.ds(pl.multiple_of(which * rows, rows), rows), col : col + HEAD_DIM]

    def entry(level, col):
        if level < 0:
            return rows_of(own, zb, col)
        if level == 0:
            near = rows_of(side, y * zb, col)
            return jnp.where(jnp.logical_and(y == 0, zb == 0), diag[:, col : col + HEAD_DIM], near)
        if level == 1:
            return jnp.where(zb == 0, rows_of(far[0], 1, col), rows_of(own, 0, col))
        return rows_of(far[level - 2], zb, col)

    factor = HEAD_DIM ** (-0.5) * math.log2(math.e)
    tile = min(256, rows)
    last = (((1,), (1,)), ((), ()))
    biases = [jnp.where(b >= 2**level, 0.0, -jnp.inf).astype(jnp.float32) for level in range(levels)]
    for g in range(heads):
        kv = g // per_kv
        ks = [entry(level, kv * HEAD_DIM) for level in range(-1, levels)]
        vs = [entry(level, kv_cols + kv * HEAD_DIM) for level in range(-1, levels)]
        for r in range(0, rows, tile):
            qt = q[r : r + tile, g * HEAD_DIM : (g + 1) * HEAD_DIM]
            seen = r + tile
            raw = lax.dot_general(qt, ks[0][:seen], last, preferred_element_type=jnp.float32)
            row_ids = lax.broadcasted_iota(jnp.int32, raw.shape, 0) + r
            col_ids = lax.broadcasted_iota(jnp.int32, raw.shape, 1)
            scores = [jnp.where(row_ids >= col_ids, raw, -jnp.inf)]
            for k, bias in zip(ks[1:], biases):
                scores.append(lax.dot_general(qt, k, last, preferred_element_type=jnp.float32) + bias)
            peak = jnp.max(scores[0], axis=1, keepdims=True)
            for score in scores[1:]:
                peak = jnp.maximum(peak, jnp.max(score, axis=1, keepdims=True))
            total = jnp.zeros((tile, 1), jnp.float32)
            summed = jnp.zeros((tile, HEAD_DIM), jnp.float32)
            for score, v in zip(scores, [vs[0][:seen]] + vs[1:]):
                expo = jnp.exp2((score - peak) * factor)
                total = total + jnp.sum(expo, axis=1, keepdims=True)
                summed = summed + jnp.dot(expo.astype(jnp.bfloat16), v, preferred_element_type=jnp.float32)
            out[r : r + tile, g * HEAD_DIM : (g + 1) * HEAD_DIM] = (summed / total).astype(out.dtype)


def attend(idx, query, own, side, diag, far, levels, per_kv):
    rows = query.shape[0] // 2
    cols = query.shape[1]
    heads = cols // HEAD_DIM

    def full(array):
        return pl.BlockSpec(array.shape, lambda i, idx: (0, 0))

    return pl.pallas_call(
        functools.partial(attend_kernel, heads, per_kv, levels),
        out_shape=jax.ShapeDtypeStruct((rows, cols), jnp.bfloat16),
        grid_spec=pltpu.PrefetchScalarGridSpec(
            num_scalar_prefetch=1,
            grid=(1,),
            in_specs=[pl.BlockSpec((rows, cols), lambda i, idx: (idx[1], 0)), full(own), full(side), full(diag)]
            + [full(f) for f in far],
            out_specs=pl.BlockSpec((rows, cols), lambda i, idx: (0, 0)),
        ),
        compiler_params=pltpu.CompilerParams(vmem_limit_bytes=40 << 20),
        cost_estimate=pl.CostEstimate(
            flops=4 * heads * (levels + 1) * rows * rows * HEAD_DIM,
            bytes_accessed=2 * (2 * rows * cols + 8 * rows * own.shape[1]),
            transcendentals=heads * (levels + 1) * rows * rows,
        ),
    )(idx, query, own, side, diag, *far)


def paired_body(tokens, w_query, w_key, w_value):
    seq_count, head_count = lax.axis_size("seq"), lax.axis_size("head")
    levels = (seq_count - 1).bit_length()
    s, h = lax.axis_index("seq"), lax.axis_index("head")
    bit = (s // 2) % 2
    rows = tokens.shape[0]
    half_kv = w_key.shape[1] // 2
    half_q = w_query.shape[1] // 2

    def half(weights, which, start, size):
        return lax.dynamic_slice_in_dim(weights, which * (weights.shape[1] // 2) + start, size, axis=1)

    stage_cols = half_q // 2
    mine, others = [], []
    for into, which in ((mine, bit), (others, 1 - bit)):
        into.append(jnp.concatenate([half(w_key, which, 0, half_kv), half(w_value, which, 0, half_kv)], axis=1))
        for part in range(2):
            into.append(half(w_query, which, part * stage_cols, stage_cols))

    xs = []
    for block in (tokens, flip(tokens, "seq", 2)):
        got = {0: block}
        mask = head_count // 2
        while mask:
            for j, piece in list(got.items()):
                got[j ^ mask] = flip(piece, "head", mask)
            mask //= 2
        xs += [got[j] for j in range(head_count)]

    def gathered(stage):
        chunks = {0: mine[stage]}
        for m in range(2, seq_count, 2):
            chunks[m] = flip((others if m & 2 else mine)[stage], "seq", m)
        for m in range(0, seq_count, 2):
            chunks[m + 1] = flip(chunks[m], "seq", 1)
        return [chunks[m] for m in range(seq_count)]

    idx = jnp.stack([s, h]).astype(jnp.int32)
    keyval = project(idx, xs, gathered(0))
    side = flip(keyval, "seq", 1)
    far = [shift(keyval, "seq", 2**level, lambda i: True) for level in range(2, levels)]
    diag = shift(keyval[rows:], "seq", 3, lambda i: i % 2 == 1)
    kept, got = [], []
    for stage in (1, 2):
        query = project(idx, xs, gathered(stage))
        per_kv = half_q // half_kv
        send, keep = (
            attend(jnp.stack([s, zb]).astype(jnp.int32), query, keyval, side, diag, far, levels, per_kv)
            for zb in (1 - bit, bit)
        )
        got.append(flip(send, "seq", 2))
        kept.append(keep)
    first = [jnp.where(bit == 0, a, b) for a, b in zip(kept, got)]
    second = [jnp.where(bit == 0, b, a) for a, b in zip(kept, got)]
    return jnp.concatenate(first + second, axis=1)


def solution(mesh):
    seq_count, head_count = mesh.shape["seq"], mesh.shape["head"]

    def power(count):
        return count & (count - 1) == 0

    def body(tokens, w_query, w_key, w_value):
        local_kv = w_key.shape[1] // HEAD_DIM
        pairs = seq_count >= 8 and power(seq_count) and power(head_count) and local_kv == 2
        return (paired_body if pairs else plain_body)(tokens, w_query, w_key, w_value)

    spec = P("seq", "head")
    return jax.shard_map(body, mesh=mesh, in_specs=(spec,) * 4, out_specs=spec, check_vma=False)
```
